512 devices in a mesh: row: 32 (over z_lo, y, core), col: 16 (over z_hi, x).
Axes of the slice: x: 4, y: 8, z: 8 (z_hi: 4, z_lo: 2; z = z_hi * 2 + z_lo), core: 2. Of those that a mesh axis runs over, the one named last changes fastest.
Arguments:
- phase: float32 [6, 524288], P(None, ('col', 'row')), may hold values from -6 to 6
- mass: float32 [524288], P(('col', 'row')), may hold values from 0.2 to 5
- active: int32 [4096], P(('row', 'col')), may hold values from 0 to 524287, as said below
Outputs:
- accels: float32 [3, 4096], P(None, ('row', 'col'))
- jerks: float32 [3, 4096], P(None, ('row', 'col'))
The draws below stay inside these ranges and needn't reach their ends.
Inputs may be any that keep to these rules, and one draw needn't show every extreme that they name: `active`: the 4096 indices are distinct.
All inputs are finite; a program needn't handle non-finite values.
Results may differ from the reference program's by a relative error of at most 0.0003.
Values sent between devices are 32-bit elements; how exact they have to be, the bound alone decides.
A program may use at most 64 MiB of HBM per device.

```python
import math
import jax
import jax.numpy as jnp
from jax import lax

NSTARS = 524288
NACT = 4096


def draw_active(key, part):
    first_key, second_key = jax.random.split(jax.random.fold_in(key, 11))
    others = 1 + jax.random.permutation(first_key, NSTARS - 2)[:NACT - 2]
    chosen = jnp.concatenate([jnp.array([0, NSTARS - 1], jnp.int32), others.astype(jnp.int32)])
    return jax.random.permutation(second_key, chosen)


def shard_levels(key, extent, cuts, low, largest):
    gain = 1.0
    for axis_at, blocks in cuts:
        draws = jax.random.uniform(jax.random.fold_in(jax.random.fold_in(key, 6), axis_at), (blocks,), jnp.float32, low / len(cuts), largest / len(cuts))
        gain = gain * jnp.repeat(jnp.exp(draws), extent[axis_at] // blocks).reshape((-1,) + (1,) * (len(extent) - 1 - axis_at))
    return gain


def normal_values(rng, shape, deviation, most, cuts=(), kind=jnp.bfloat16):
    values = jax.random.normal(rng, shape, jnp.float32) * deviation
    if len(cuts) > 0:
        values = shard_levels(rng, shape, cuts, -0.22, 0.18) * values
    return jnp.clip(values, min=-most, max=most).astype(kind)


def setup_inputs(seed: int = 0) -> dict:
    keys = jax.random.split(jax.random.key(seed), 4)
    phase = normal_values(keys[0], (6, NSTARS), 1.0, 6.0, ((1, 512),), jnp.float32)
    mass = jnp.clip(jnp.exp(math.log(5.0) - 3.218876 * jax.random.uniform(keys[1], (NSTARS,), jnp.float32) ** shard_levels(keys[1], (NSTARS,), ((0, 512),), -0.2, 0.2)), 0.2, 5.0)
    active = draw_active(jax.random.fold_in(keys[3], 71), 0)
    return dict(phase=phase, mass=mass, active=active)


SOFTENING = 0.0001

def pair_terms(targets, src_phase, src_mass):
    offset = src_phase[0:3, None, :] - targets[0:3, :, None]
    vel_diff = src_phase[3:6, None, :] - targets[3:6, :, None]
    dist_sq = lax.optimization_barrier(jnp.sum(offset * offset, axis=0)) + SOFTENING
    inverse = lax.rsqrt(dist_sq)
    inverse_sq = inverse * inverse
    weight = src_mass[None, :] * inverse * inverse_sq
    radial = 3.0 * lax.optimization_barrier(jnp.sum(offset * vel_diff, axis=0)) * inverse_sq
    accels = lax.optimization_barrier(jnp.sum(weight[None] * offset, axis=-1))
    jerks = lax.optimization_barrier(jnp.sum(weight[None] * (vel_diff - radial[None] * offset), axis=-1))
    return (accels, jerks)

def reference(phase, mass, active):
    targets = jnp.take(phase, active.astype(jnp.int32), axis=1)
    block_len = math.gcd(NSTARS, 512)
    block_count = NSTARS // block_len

    def add_block(carry, counter):
        first = (counter * block_len).astype(jnp.int32)
        src_phase = lax.dynamic_slice_in_dim(phase, first, block_len, 1)
        src_mass = lax.dynamic_slice_in_dim(mass, first, block_len, 0)
        accels, jerks = pair_terms(targets, src_phase, src_mass)
        return ((carry[0] + accels, carry[1] + jerks), None)
    zeros = jnp.zeros((3, NACT), jnp.float32)
    totals, unused = lax.scan(add_block, (zeros, zeros), jnp.arange(block_count, dtype=jnp.int32))
    return (totals[0] * (1.0 / NSTARS), totals[1] * (1.0 / NSTARS))
```

```python
import functools

import jax
import jax.numpy as jnp
from jax import lax
from jax.experimental import pallas as pl
from jax.experimental.pallas import tpu as pltpu
from jax.sharding import PartitionSpec as P

SOFTENING = 0.0001
MESH = pl.DeviceIdType.MESH

NX, NY, NZ = 4, 8, 8
SRC_GROUP = NY * 2
TGT_GROUP = NX * NZ
STARS = 1024
TILES = STARS // 128
MINE = 8
PAIRS = TGT_GROUP // 2


def remote(src, dst, send, recv, device):
    return pltpu.make_async_remote_copy(
        src_ref=src, dst_ref=dst, send_sem=send, recv_sem=recv, device_id=device, device_id_type=MESH
    )


def kernel(
    norming, phase_ref, mass_ref, active_ref, acc_out, jerk_out,
    src, msrc, idx_x, idx_z, pick_x, pick_z, tgt, stage, part,
    own_sem, src_send, src_recv, mass_send, mass_recv, ix_send, ix_recv, iz_send, iz_recv,
    px_send, px_recv, pz_send, pz_recv, fin_send, fin_recv,
):
    r, c = lax.axis_index("row"), lax.axis_index("col")
    z_lo, b = r // 16, r % 16
    y, core = b // 2, b % 2
    z_hi, x = c // NX, c % NX
    z = z_hi * 2 + z_lo
    m = z_lo * 16 + c
    lane = lax.broadcasted_iota(jnp.int32, (8, 128), 1)

    def at_y(k, other):
        yy = (y + k) % NY
        cc = 1 - core if other else core
        return (z_lo * 16 + yy * 2 + cc, c)

    def at_x(k):
        return (r, z_hi * NX + (x + k) % NX)

    def at_z(k):
        zz = (z + k) % NZ
        return ((zz % 2) * 16 + b, (zz // 2) * NX + x)

    sources = [at_y(k, o) for o in (False, True) for k in range(NY) if o or k]
    partners = sources + [at_x(k) for k in range(1, NX)] + [at_z(k) for k in range(1, NZ)]
    barrier = pltpu.get_barrier_semaphore()
    for device in partners:
        pl.semaphore_signal(barrier, inc=1, device_id=device, device_id_type=MESH)

    own = [
        pltpu.make_async_copy(phase_ref, src.at[b], own_sem.at[0]),
        pltpu.make_async_copy(mass_ref, msrc.at[b], own_sem.at[1]),
    ]
    for copy in own:
        copy.start()
    idx_x[x] = jnp.zeros((8, 128), jnp.int32)
    idx_x[x, 0:1, 0:MINE] = active_ref[...]
    row = idx_x[x, 0:1, :]
    for shift in (8, 16, 32, 64):
        row = row + pltpu.roll(row, shift, 1)
    idx_x[x] = jnp.broadcast_to(row, (8, 128))

    pl.semaphore_wait(barrier, len(partners))

    sends = []

    def go(copy):
        copy.start()
        sends.append(copy)

    for n, k in enumerate((4, 3, 5, 2, 6, 1, 7)):
        go(remote(phase_ref, src.at[b], src_send.at[n], src_recv.at[b], at_y(k, False)))
    go(remote(phase_ref, src.at[b], src_send.at[7], src_recv.at[b], at_y(0, True)))
    for k in range(1, NX):
        go(remote(idx_x.at[x], idx_x.at[x], ix_send.at[k], ix_recv.at[x], at_x(k)))
    for n, device in enumerate(sources):
        go(remote(mass_ref, msrc.at[b], mass_send.at[n], mass_recv.at[b], device))

    merged = jnp.where((lane // 8) % NX == x, idx_x[x], 0)
    for k in range(1, NX):
        xx = (x + k) % NX
        remote(idx_x.at[xx], idx_x.at[xx], ix_send.at[0], ix_recv.at[xx], at_x(k)).wait_recv()
        merged = jnp.where((lane // 8) % NX == xx, idx_x[xx], merged)
    idx_z[z] = merged
    for k in range(1, NZ):
        go(remote(idx_z.at[z], idx_z.at[z], iz_send.at[k], iz_recv.at[z], at_z(k)))

    for n, k in enumerate((1, 7, 2, 6, 3, 5, 4)):
        bb = ((y + k) % NY) * 2 + core
        remote(phase_ref, src.at[bb], src_send.at[0], src_recv.at[bb], at_y(k, False)).wait_recv()
        go(remote(src.at[bb], src.at[bb], src_send.at[8 + n], src_recv.at[bb], at_y(0, True)))
    for k in range(1, NZ):
        zz = (z + k) % NZ
        remote(idx_z.at[zz], idx_z.at[zz], iz_send.at[0], iz_recv.at[zz], at_z(k)).wait_recv()
    base = (c * 32 + z_lo * 16) * STARS
    offset = []
    for q in range(2):
        index = jnp.zeros((8, 128), jnp.int32)
        for h in range(NZ // 2):
            index = jnp.where(lane // 32 == h, idx_z[h * 2 + q], index)
        offset.append(index - base)
    for copy in own:
        copy.wait()
    for k in range(NY):
        bb = ((y + k) % NY) * 2 + 1 - core
        remote(phase_ref, src.at[bb], src_send.at[0], src_recv.at[bb], at_y(0, True)).wait_recv()

    within = [o % 128 for o in offset]
    tile = [lax.shift_right_arithmetic(o, 7) for o in offset]

    def pick(bb, found):
        found = list(found)
        for k in range(TILES):
            piece = src[bb, :, k * 128:(k + 1) * 128]
            for q in range(2):
                values = jnp.take_along_axis(piece, within[q][:6], axis=1)
                found[q] = jnp.where(tile[q][:6] == bb * TILES + k, values, found[q])
        return tuple(found)

    nothing = jnp.zeros((6, 128), jnp.float32)
    found = lax.fori_loop(0, SRC_GROUP, pick, (nothing, nothing))
    for q in range(2):
        pick_x[x, q] = found[q]
    for k in range(1, NX):
        go(remote(pick_x.at[x], pick_x.at[x], px_send.at[k], px_recv.at[x], at_x(k)))
    total = list(found)
    for k in range(1, NX):
        xx = (x + k) % NX
        remote(pick_x.at[xx], pick_x.at[xx], px_send.at[0], px_recv.at[xx], at_x(k)).wait_recv()
        for q in range(2):
            total[q] = total[q] + pick_x[xx, q]
    for q in range(2):
        pick_z[z, q] = total[q]
    for k in range(1, NZ):
        go(remote(pick_z.at[z], pick_z.at[z], pz_send.at[k], pz_recv.at[z], at_z(k)))
    for k in (1, 7, 2, 6, 3, 5, 4):
        zz = (z + k) % NZ
        remote(pick_z.at[zz], pick_z.at[zz], pz_send.at[0], pz_recv.at[zz], at_z(k)).wait_recv()
        for q in range(2):
            total[q] = total[q] + pick_z[zz, q]
    for q in range(2):
        turned = jnp.concatenate([total[q], jnp.zeros((2, 128), jnp.float32)], axis=0).T
        for k in range(6):
            tgt[k, q * 128:(q + 1) * 128, :] = jnp.broadcast_to(turned[:, k:k + 1], (128, 128))
    for n in range(15):
        k, other = (n + 1, False) if n < 7 else (n - 7, True)
        bb = ((y + k) % NY) * 2 + (1 - core if other else core)
        remote(mass_ref, msrc.at[bb], mass_send.at[0], mass_recv.at[bb], at_y(k, other)).wait_recv()

    def block(i, carry):
        step = i // 2
        zz = (z + 4 + (1 - 2 * (step % 2)) * ((step + 1) // 2)) % NZ
        half = (x // 2 + 1 + i) % 2
        p = (zz % 2) * 8 + (zz // 2) * 2 + half
        first = pl.multiple_of(p * 16, 16)
        here = [[tgt[k, pl.ds(first + 8 * g, 8), :] for k in range(6)] for g in range(2)]

        def sweep(bb, sums):
            sums = [list(s) for s in sums]
            for k in range(TILES):
                star = [jnp.broadcast_to(src[bb, n:n + 1, k * 128:(k + 1) * 128], (8, 128)) for n in range(6)]
                heft = jnp.broadcast_to(msrc[bb, k:k + 1, :], (8, 128))
                for g in range(2):
                    dx, dy, dz, du, dv, dw = (star[n] - here[g][n] for n in range(6))
                    dist_sq = (dx * dx + dy * dy + dz * dz) + SOFTENING
                    inverse = lax.rsqrt(dist_sq)
                    inverse_sq = inverse * inverse
                    weight = heft * inverse * inverse_sq
                    radial = 3.0 * (dx * du + dy * dv + dz * dw) * inverse_sq
                    s = sums[g]
                    s[0] += weight * dx
                    s[1] += weight * dy
                    s[2] += weight * dz
                    s[3] += weight * (du - radial * dx)
                    s[4] += weight * (dv - radial * dy)
                    s[5] += weight * (dw - radial * dz)
            return tuple(tuple(s) for s in sums)

        zero = jnp.zeros((8, 128), jnp.float32)
        sums = lax.fori_loop(0, SRC_GROUP, sweep, ((zero,) * 6,) * 2)
        for g in range(2):
            out = zero
            for n in range(6):
                out = jnp.where(lane == n, jnp.sum(sums[g][n], axis=1, keepdims=True), out)
            member = p * 2 + g
            stage[member] = out

            @pl.when(member != m)
            def _():
                device = ((zz % 2) * 16 + b, (zz // 2) * NX + half * 2 + g)
                remote(stage.at[member], part.at[m], fin_send.at[member], fin_recv.at[m], device).start()

        return carry

    lax.fori_loop(0, PAIRS, block, 0)

    def gather(k, carry):
        member = (m + k) % TGT_GROUP
        remote(stage.at[member], part.at[member], fin_send.at[member], fin_recv.at[member], at_x(1)).wait()
        return carry

    lax.fori_loop(1, TGT_GROUP, gather, 0)
    out = stage[m]
    for k in range(1, TGT_GROUP):
        out = out + part[(m + k) % TGT_GROUP]
    turned = (out * norming).T
    acc_out[...] = turned[0:3, :]
    jerk_out[...] = turned[3:6, :]
    for copy in sends:
        copy.wait_send()


def shards(phase, mass, active):
    count = phase.shape[1] * lax.axis_size("row") * lax.axis_size("col")
    vmem = pl.BlockSpec(memory_space=pltpu.VMEM)
    hbm = pl.BlockSpec(memory_space=pl.ANY)
    dma = pltpu.SemaphoreType.DMA
    out = jax.ShapeDtypeStruct((3, MINE), jnp.float32)
    return pl.pallas_call(
        functools.partial(kernel, 1.0 / count),
        out_shape=(out, out),
        in_specs=[hbm, hbm, vmem],
        out_specs=(vmem, vmem),
        scratch_shapes=[
            pltpu.VMEM((SRC_GROUP, 6, STARS), jnp.float32),
            pltpu.VMEM((SRC_GROUP, TILES, 128), jnp.float32),
            pltpu.VMEM((NX, 8, 128), jnp.int32),
            pltpu.VMEM((NZ, 8, 128), jnp.int32),
            pltpu.VMEM((NX, 2, 6, 128), jnp.float32),
            pltpu.VMEM((NZ, 2, 6, 128), jnp.float32),
            pltpu.VMEM((6, TGT_GROUP * MINE, 128), jnp.float32),
            pltpu.VMEM((TGT_GROUP, 8, 128), jnp.float32),
            pltpu.VMEM((TGT_GROUP, 8, 128), jnp.float32),
            dma((2,)),
            dma((15,)),
            dma((SRC_GROUP,)),
            dma((15,)),
            dma((SRC_GROUP,)),
            dma((NX,)),
            dma((NX,)),
            dma((NZ,)),
            dma((NZ,)),
            dma((NX,)),
            dma((NX,)),
            dma((NZ,)),
            dma((NZ,)),
            dma((TGT_GROUP,)),
            dma((TGT_GROUP,)),
        ],
        compiler_params=pltpu.CompilerParams(collective_id=0, has_side_effects=True),
    )(phase, mass.reshape(TILES, 128), active.reshape(1, MINE))


def solution(mesh):
    in_specs = (P(None, ("col", "row")), P(("col", "row")), P(("row", "col")))
    out_specs = (P(None, ("row", "col")), P(None, ("row", "col")))
    return jax.shard_map(shards, mesh=mesh, in_specs=in_specs, out_specs=out_specs, check_vma=False)
```

```python
import jax
import jax.numpy as jnp
from jax import lax
from jax.experimental import pallas as pl
from jax.experimental.pallas import tpu as pltpu
from jax.sharding import PartitionSpec as P

SOFTENING = 0.0001
MESH = pl.DeviceIdType.MESH

NX, NY, NZ = 4, 8, 8
SRC_GROUP = NX * 2 * 2
TGT_GROUP = NY // 2 * NZ
STARS = 1024
TILES = STARS // 128
MINE = 8
PAIRS = TGT_GROUP // 2


def remote(src, dst, send, recv, device):
    return pltpu.make_async_remote_copy(
        src_ref=src, dst_ref=dst, send_sem=send, recv_sem=recv, device_id=device, device_id_type=MESH
    )


def kernel(
    phase_ref, mass_ref, active_ref, out_ref,
    src, msrc, ids, idx, pick, tgt, stage, part,
    own_sem, src_send, src_recv, mass_send, mass_recv, idx_send, idx_recv, pick_send, pick_recv, fin_send, fin_recv,
):
    r, c = lax.axis_index("row"), lax.axis_index("col")
    z_lo, y, core = r // 16, r // 2 % 8, r % 2
    z_hi, x = c // NX, c % NX
    z, y_hi, y_lo = z_hi * 2 + z_lo, y // 2, y % 2
    b = x * 4 + y_lo * 2 + core
    m = y_hi * NZ + z
    lane = lax.broadcasted_iota(jnp.int32, (8, 128), 1)

    def place(xx, yy, zz, cc):
        return ((zz % 2) * 16 + yy * 2 + cc, (zz // 2) * NX + xx)

    def source(dx, dy, dc):
        xx, yl, cc = (x + dx) % NX, (y_lo + dy) % 2, (core + dc) % 2
        return place(xx, y_hi * 2 + yl, z, cc), xx * 4 + yl * 2 + cc

    def target(dy, dz):
        yh, zz = (y_hi + dy) % (NY // 2), (z + dz) % NZ
        return place(x, yh * 2 + y_lo, zz, core), yh * NZ + zz

    near = [source(dx, dy, 0) for dx, dy in ((2, 1), (1, 1), (3, 1), (2, 0), (1, 0), (3, 0), (0, 1))]
    twin, twin_block = source(0, 0, 1)
    beyond = [source(dx, dy, 1) for dx, dy in ((2, 1), (1, 1), (3, 1), (2, 0), (1, 0), (3, 0), (0, 1))]
    fellows = [target(dy, dz) for dy in (2, 1, 3, 0) for dz in (4, 3, 5, 2, 6, 1, 7, 0) if dy or dz]
    partners = [d for d, _ in near + beyond + fellows] + [twin]
    barrier = pltpu.get_barrier_semaphore()
    for device in partners:
        pl.semaphore_signal(barrier, inc=1, device_id=device, device_id_type=MESH)

    own = [
        pltpu.make_async_copy(active_ref, ids, own_sem.at[0]),
        pltpu.make_async_copy(phase_ref, src.at[b], own_sem.at[1]),
        pltpu.make_async_copy(mass_ref, msrc.at[b], own_sem.at[2]),
    ]
    for copy in own:
        copy.start()
    own[0].wait()
    idx[m] = jnp.zeros((1, 128), jnp.int32)
    idx[m, :, 0:MINE] = ids[...]
    row = idx[m]
    for shift in (8, 16, 32, 64):
        row = row + pltpu.roll(row, shift, 1)
    idx[m] = row

    pl.semaphore_wait(barrier, len(partners))

    sends = []

    def go(copy):
        copy.start()
        sends.append(copy)

    for n, (device, _) in enumerate(near + [(twin, 0)]):
        go(remote(phase_ref, src.at[b], src_send.at[n], src_recv.at[b], device))
    for n, (device, _) in enumerate(fellows):
        go(remote(idx.at[m], idx.at[m], idx_send.at[n], idx_recv.at[m], device))
    for n, (device, _) in enumerate(near + beyond + [(twin, 0)]):
        go(remote(mass_ref, msrc.at[b], mass_send.at[n], mass_recv.at[b], device))

    for n in (6, 5, 4, 3, 2, 1, 0):
        device, bb = near[n]
        remote(phase_ref, src.at[bb], src_send.at[0], src_recv.at[bb], device).wait_recv()
        go(remote(src.at[bb], src.at[bb], src_send.at[8 + n], src_recv.at[bb], twin))
    for device, mm in fellows:
        remote(idx.at[mm], idx.at[mm], idx_send.at[0], idx_recv.at[mm], device).wait_recv()

    within, tile = [], []
    for q in range(2):
        index = jnp.zeros((8, 128), jnp.int32)
        for g in range(16):
            index = jnp.where(lane // MINE == g, jnp.broadcast_to(idx[q * 16 + g], (8, 128)), index)
        index = index[:6]
        block = index // STARS
        here = (block // 128 == z_hi) & (block // 16 % 2 == z_lo) & (block // 4 % 4 == y_hi)
        within.append(index % 128)
        tile.append(jnp.where(here, (block // 32 % 4 * 4 + block % 4) * TILES + index // 128 % TILES, -1))
    for copy in own[1:]:
        copy.wait()
    for device, bb in [(twin, twin_block)] + beyond[::-1]:
        remote(phase_ref, src.at[bb], src_send.at[0], src_recv.at[bb], twin).wait_recv()

    def choose(bb, found):
        found = list(found)
        for k in range(TILES):
            piece = src[bb, :, k * 128:(k + 1) * 128]
            for q in range(2):
                values = jnp.take_along_axis(piece, within[q], axis=1)
                found[q] = jnp.where(tile[q] == bb * TILES + k, values, found[q])
        return tuple(found)

    nothing = jnp.zeros((6, 128), jnp.float32)
    found = lax.fori_loop(0, SRC_GROUP, choose, (nothing, nothing))
    for q in range(2):
        pick[m, q] = found[q]
    for n, (device, _) in enumerate(fellows):
        go(remote(pick.at[m], pick.at[m], pick_send.at[n], pick_recv.at[m], device))
    for n, (device, bb) in enumerate(near + beyond + [(twin, twin_block)]):
        remote(mass_ref, msrc.at[bb], mass_send.at[0], mass_recv.at[bb], device).wait_recv()
    total = list(found)
    for device, mm in fellows[::-1]:
        remote(pick.at[mm], pick.at[mm], pick_send.at[0], pick_recv.at[mm], device).wait_recv()
        for q in range(2):
            total[q] = total[q] + pick[mm, q]
    for q in range(2):
        turned = jnp.concatenate([total[q], jnp.zeros((2, 128), jnp.float32)], axis=0).T
        for k in range(6):
            tgt[k, q * 128:(q + 1) * 128, :] = jnp.broadcast_to(turned[:, k:k + 1], (128, 128))

    def block(i, carry):
        def far(j):
            return 2 + j // 2 - (j % 2) * (1 + 2 * (j // 2))

        yh, zp = (y_hi + far(i // 4)) % 4, (z // 2 + far(i % 4)) % 4
        p = yh * 4 + zp
        first = pl.multiple_of(p * 16, 16)
        here = [[tgt[k, pl.ds(first + 8 * g, 8), :] for k in range(6)] for g in range(2)]

        def sweep(bb, sums):
            sums = [list(s) for s in sums]
            for k in range(TILES):
                star = [jnp.broadcast_to(src[bb, n:n + 1, k * 128:(k + 1) * 128], (8, 128)) for n in range(6)]
                heft = jnp.broadcast_to(msrc[bb, k:k + 1, :], (8, 128))
                for g in range(2):
                    dx, dy, dz, du, dv, dw = (star[n] - here[g][n] for n in range(6))
                    dist_sq = (dx * dx + dy * dy + dz * dz) + SOFTENING
                    inverse = lax.rsqrt(dist_sq)
                    inverse_sq = inverse * inverse
                    weight = heft * inverse * inverse_sq
                    radial = 3.0 * (dx * du + dy * dv + dz * dw) * inverse_sq
                    s = sums[g]
                    s[0] += weight * dx
                    s[1] += weight * dy
                    s[2] += weight * dz
                    s[3] += weight * (du - radial * dx)
                    s[4] += weight * (dv - radial * dy)
                    s[5] += weight * (dw - radial * dz)
            return tuple(tuple(s) for s in sums)

        zero = jnp.zeros((8, 128), jnp.float32)
        sums = lax.fori_loop(0, SRC_GROUP, sweep, ((zero,) * 6,) * 2)
        for g in range(2):
            out = zero
            for n in range(6):
                out = jnp.where(lane == n, jnp.sum(sums[g][n], axis=1, keepdims=True), out)
            member = p * 2 + g
            stage[member] = out

            @pl.when(member != m)
            def _():
                device = place(x, yh * 2 + y_lo, zp * 2 + g, core)
                remote(stage.at[member], part.at[m], fin_send.at[member], fin_recv.at[m], device).start()

        return carry

    lax.fori_loop(0, PAIRS, block, 0)

    def gather(k, carry):
        member = (m + k) % TGT_GROUP
        remote(stage.at[member], part.at[member], fin_send.at[member], fin_recv.at[member], twin).wait()
        return carry

    lax.fori_loop(1, TGT_GROUP, gather, 0)
    out = stage[m]
    for k in range(1, TGT_GROUP):
        out = out + part[(m + k) % TGT_GROUP]
    out_ref[...] = out.T[0:8, :]
    for copy in sends:
        copy.wait_send()


def shards(phase, mass, active):
    norming = 1.0 / (phase.shape[1] * lax.axis_size("row") * lax.axis_size("col"))
    vmem = pl.BlockSpec(memory_space=pltpu.VMEM)
    hbm = pl.BlockSpec(memory_space=pl.ANY)
    dma = pltpu.SemaphoreType.DMA
    sums = pl.pallas_call(
        kernel,
        out_shape=jax.ShapeDtypeStruct((8, MINE), jnp.float32),
        in_specs=[hbm, hbm, hbm],
        out_specs=vmem,
        scratch_shapes=[
            pltpu.VMEM((SRC_GROUP, 6, STARS), jnp.float32),
            pltpu.VMEM((SRC_GROUP, TILES, 128), jnp.float32),
            pltpu.VMEM((1, MINE), jnp.int32),
            pltpu.VMEM((TGT_GROUP, 1, 128), jnp.int32),
            pltpu.VMEM((TGT_GROUP, 2, 6, 128), jnp.float32),
            pltpu.VMEM((6, TGT_GROUP * MINE, 128), jnp.float32),
            pltpu.VMEM((TGT_GROUP, 8, 128), jnp.float32),
            pltpu.VMEM((TGT_GROUP, 8, 128), jnp.float32),
            dma((3,)),
            dma((15,)),
            dma((SRC_GROUP,)),
            dma((15,)),
            dma((SRC_GROUP,)),
            dma((TGT_GROUP,)),
            dma((TGT_GROUP,)),
            dma((TGT_GROUP,)),
            dma((TGT_GROUP,)),
            dma((TGT_GROUP,)),
            dma((TGT_GROUP,)),
        ],
        compiler_params=pltpu.CompilerParams(collective_id=0, has_side_effects=True),
    )(phase, mass.reshape(TILES, 128), active.reshape(1, MINE))
    return sums[0:3] * norming, sums[3:6] * norming


def solution(mesh):
    in_specs = (P(None, ("col", "row")), P(("col", "row")), P(("row", "col")))
    out_specs = (P(None, ("row", "col")), P(None, ("row", "col")))
    return jax.shard_map(shards, mesh=mesh, in_specs=in_specs, out_specs=out_specs, check_vma=False)
```

```python
import jax
import jax.numpy as jnp
from jax import lax
from jax.experimental import pallas as pl
from jax.experimental.pallas import tpu as pltpu
from jax.sharding import PartitionSpec as P

SOFTENING = 0.0001
MESH = pl.DeviceIdType.MESH

NX, NY, NZ = 4, 8, 8
SRC_GROUP = NY * 2
TGT_GROUP = NX * NZ
STARS = 1024
TILES = STARS // 128
MINE = 8
PAIRS = TGT_GROUP // 2


def remote(src, dst, send, recv, device):
    return pltpu.make_async_remote_copy(
        src_ref=src, dst_ref=dst, send_sem=send, recv_sem=recv, device_id=device, device_id_type=MESH
    )


def kernel(
    phase_ref, mass_ref, active_ref, out_ref,
    src, msrc, ids, idx_x, idx_z, pick_x, pick_z, tgt, raw, stage, part,
    own_sem, src_send, src_recv, mass_send, mass_recv, ix_send, ix_recv, iz_send, iz_recv,
    px_send, px_recv, pz_send, pz_recv, fin_send, fin_recv,
):
    r, c = lax.axis_index("row"), lax.axis_index("col")
    z_lo, b = r // 16, r % 16
    y, core = b // 2, b % 2
    z_hi, x = c // NX, c % NX
    z = z_hi * 2 + z_lo
    m = z_lo * 16 + c
    slot = core * NX + x
    lane = lax.broadcasted_iota(jnp.int32, (8, 128), 1)

    def along_y(k, dc):
        bb = (y + k) % NY * 2 + (core + dc) % 2
        return (z_lo * 16 + bb, c), bb

    def along_x(k, dc):
        xx, cc = (x + k) % NX, (core + dc) % 2
        return (z_lo * 16 + y * 2 + cc, z_hi * NX + xx), cc * NX + xx

    def along_z(k):
        zz = (z + k) % NZ
        return (zz % 2 * 16 + b, zz // 2 * NX + x), zz

    near = [along_y(k, 0) for k in (4, 3, 5, 2, 6, 1, 7)]
    beyond = [along_y(k, 1) for k in (4, 3, 5, 2, 6, 1, 7)]
    twin, twin_block = along_y(0, 1)
    across = [along_x(k, dc) for k, dc in ((2, 1), (2, 0), (1, 1), (3, 1), (1, 0), (3, 0), (0, 1))]
    fellows = [along_z(k) for k in (4, 3, 5, 2, 6, 1, 7)]
    partners = [d for d, _ in near + beyond + across + fellows]
    barrier = pltpu.get_barrier_semaphore()
    for device in partners:
        pl.semaphore_signal(barrier, inc=1, device_id=device, device_id_type=MESH)

    own = [
        pltpu.make_async_copy(active_ref, ids, own_sem.at[0]),
        pltpu.make_async_copy(phase_ref, src.at[b], own_sem.at[1]),
        pltpu.make_async_copy(mass_ref, msrc.at[b], own_sem.at[2]),
    ]
    for copy in own:
        copy.start()
    own[0].wait()
    idx_x[slot] = jnp.zeros((8, 128), jnp.int32)
    idx_x[slot, 0:1, 0:MINE] = ids[...]
    row = idx_x[slot, 0:1, :]
    for shift in (8, 16, 32, 64):
        row = row + pltpu.roll(row, shift, 1)
    idx_x[slot] = jnp.broadcast_to(row, (8, 128))

    pl.semaphore_wait(barrier, len(partners))

    sends = []

    def go(copy):
        copy.start()
        sends.append(copy)

    for n, (device, _) in enumerate(near):
        go(remote(phase_ref, src.at[b], src_send.at[n], src_recv.at[b], device))
    for n, (device, _) in enumerate(across):
        go(remote(idx_x.at[slot], idx_x.at[slot], ix_send.at[n], ix_recv.at[slot], device))
    go(remote(phase_ref, src.at[b], src_send.at[7], src_recv.at[b], twin))
    for n, (device, _) in enumerate(near + beyond + [(twin, 0)]):
        go(remote(mass_ref, msrc.at[b], mass_send.at[n], mass_recv.at[b], device))

    for device, ss in across:
        remote(idx_x.at[ss], idx_x.at[ss], ix_send.at[0], ix_recv.at[ss], device).wait_recv()
    sublane = lax.broadcasted_iota(jnp.int32, (8, 128), 0)
    merged = jnp.zeros((8, 128), jnp.int32)
    for cc in range(2):
        for xx in range(NX):
            chosen = (lane // MINE % NX == xx) & ((sublane == 0) == (cc == 0))
            merged = jnp.where(chosen, idx_x[cc * NX + xx], merged)
    idx_z[z] = merged
    for n, (device, _) in enumerate(fellows):
        go(remote(idx_z.at[z], idx_z.at[z], iz_send.at[n], iz_recv.at[z], device))
    for device, zz in fellows:
        remote(idx_z.at[zz], idx_z.at[zz], iz_send.at[0], iz_recv.at[zz], device).wait_recv()

    base = (c * 32 + z_lo * 16) * STARS
    within, tile = [], []
    for cc in range(2):
        for q in range(2):
            index = jnp.zeros((6, 128), jnp.int32)
            for h in range(NZ // 2):
                ids_h = jnp.broadcast_to(idx_z[h * 2 + q, cc:cc + 1, :], (6, 128))
                index = jnp.where(lane[:6] // 32 == h, ids_h, index)
            within.append((index - base) % 128)
            tile.append(lax.shift_right_arithmetic(index - base, 7))

    for n in (5, 6, 3, 4, 1, 2, 0):
        device, bb = near[n]
        remote(phase_ref, src.at[bb], src_send.at[0], src_recv.at[bb], device).wait_recv()
        go(remote(src.at[bb], src.at[bb], src_send.at[8 + n], src_recv.at[bb], twin))
    for copy in own[1:]:
        copy.wait()

    def choose(yy, found):
        found = list(found)
        bb = yy * 2 + core
        for k in range(TILES):
            piece = src[bb, :, k * 128:(k + 1) * 128]
            for n in range(4):
                values = jnp.take_along_axis(piece, within[n], axis=1)
                found[n] = jnp.where(tile[n] == bb * TILES + k, values, found[n])
        return tuple(found)

    found = lax.fori_loop(0, NY, choose, (jnp.zeros((6, 128), jnp.float32),) * 4)
    for n in range(4):
        pick_x[n // 2, slot, n % 2] = found[n]
    for n, (device, ss) in enumerate(across):
        cc = ss // NX
        go(remote(pick_x.at[cc, slot], pick_x.at[cc, slot], px_send.at[n], px_recv.at[slot], device))
    total = [pick_x[core, slot, q] for q in range(2)]
    for device, ss in across[::-1]:
        remote(pick_x.at[core, ss], pick_x.at[core, ss], px_send.at[0], px_recv.at[ss], device).wait_recv()
        for q in range(2):
            total[q] = total[q] + pick_x[core, ss, q]
    for q in range(2):
        pick_z[z, q] = total[q]
    for n, (device, _) in enumerate(fellows):
        go(remote(pick_z.at[z], pick_z.at[z], pz_send.at[n], pz_recv.at[z], device))
    for device, bb in [(twin, twin_block)] + beyond:
        remote(phase_ref, src.at[bb], src_send.at[0], src_recv.at[bb], twin).wait_recv()
    for device, bb in near + beyond + [(twin, twin_block)]:
        remote(mass_ref, msrc.at[bb], mass_send.at[0], mass_recv.at[bb], device).wait_recv()
    for device, zz in fellows[::-1]:
        remote(pick_z.at[zz], pick_z.at[zz], pz_send.at[0], pz_recv.at[zz], device).wait_recv()
        for q in range(2):
            total[q] = total[q] + pick_z[zz, q]
    for q in range(2):
        turned = jnp.concatenate([total[q], jnp.zeros((2, 128), jnp.float32)], axis=0).T
        for k in range(6):
            tgt[k, q * 128:(q + 1) * 128, :] = jnp.broadcast_to(turned[:, k:k + 1], (128, 128))

    def pair(i):
        step = i // 2
        zz = (z + 4 + (1 - 2 * (step % 2)) * ((step + 1) // 2)) % NZ
        half = (x // 2 + 1 + i) % 2
        return zz, half, zz % 2 * 8 + zz // 2 * 2 + half

    def reduce(p):
        for g in range(2):
            out = jnp.zeros((8, 128), jnp.float32)
            for n in range(6):
                out = jnp.where(lane == n, jnp.sum(raw[g, n], axis=1, keepdims=True), out)
            stage[p * 2 + g] = out

    def hand_over(zz, half, p, g):
        device = (zz % 2 * 16 + b, zz // 2 * NX + half * 2 + g)
        remote(stage.at[p * 2 + g], part.at[m], fin_send.at[p * 2 + g], fin_recv.at[m], device).start()

    def block(i, carry):
        p = pair(i)[2]
        before = pair(jnp.maximum(i - 1, 0))
        first = pl.multiple_of(p * 16, 16)
        here = [[tgt[k, pl.ds(first + 8 * g, 8), :] for k in range(6)] for g in range(2)]
        reduce(before[2])
        zero = jnp.zeros((8, 128), jnp.float32)
        sums = [[zero] * 6, [zero] * 6]
        for t in range(SRC_GROUP * TILES):
            bb, k = t // TILES, t % TILES
            star = [jnp.broadcast_to(src[bb, n:n + 1, k * 128:(k + 1) * 128], (8, 128)) for n in range(6)]
            heft = jnp.broadcast_to(msrc[bb, k:k + 1, :], (8, 128))
            for g in range(2):
                dx, dy, dz, du, dv, dw = (star[n] - here[g][n] for n in range(6))
                dist_sq = (dx * dx + dy * dy + dz * dz) + SOFTENING
                inverse = lax.rsqrt(dist_sq)
                inverse_sq = inverse * inverse
                weight = heft * inverse * inverse_sq
                radial = 3.0 * (dx * du + dy * dv + dz * dw) * inverse_sq
                s = sums[g]
                s[0] += weight * dx
                s[1] += weight * dy
                s[2] += weight * dz
                s[3] += weight * (du - radial * dx)
                s[4] += weight * (dv - radial * dy)
                s[5] += weight * (dw - radial * dz)
        for g in range(2):
            for n in range(6):
                raw[g, n] = sums[g][n]

        @pl.when(i > 0)
        def _():
            for g in range(2):
                hand_over(*before, g)

        return carry

    raw[...] = jnp.zeros_like(raw)
    lax.fori_loop(0, PAIRS, block, 0)
    zz, half, p = pair(PAIRS - 1)
    reduce(p)
    for g in range(2):
        @pl.when(x % 2 != g)
        def _():
            hand_over(zz, half, p, g)

    def gather(k, carry):
        member = (m + k) % TGT_GROUP
        remote(stage.at[member], part.at[member], fin_send.at[member], fin_recv.at[member], twin).wait()
        return carry

    lax.fori_loop(1, TGT_GROUP, gather, 0)
    out = stage[m]
    for k in range(1, TGT_GROUP):
        out = out + part[(m + k) % TGT_GROUP]
    out_ref[...] = out.T[0:8, :]
    for copy in sends:
        copy.wait_send()


def shards(phase, mass, active):
    norming = 1.0 / (phase.shape[1] * lax.axis_size("row") * lax.axis_size("col"))
    vmem = pl.BlockSpec(memory_space=pltpu.VMEM)
    hbm = pl.BlockSpec(memory_space=pl.ANY)
    dma = pltpu.SemaphoreType.DMA
    sums = pl.pallas_call(
        kernel,
        out_shape=jax.ShapeDtypeStruct((8, MINE), jnp.float32),
        in_specs=[hbm, hbm, hbm],
        out_specs=vmem,
        scratch_shapes=[
            pltpu.VMEM((SRC_GROUP, 6, STARS), jnp.float32),
            pltpu.VMEM((SRC_GROUP, TILES, 128), jnp.float32),
            pltpu.VMEM((1, MINE), jnp.int32),
            pltpu.VMEM((2 * NX, 8, 128), jnp.int32),
            pltpu.VMEM((NZ, 8, 128), jnp.int32),
            pltpu.VMEM((2, 2 * NX, 2, 6, 128), jnp.float32),
            pltpu.VMEM((NZ, 2, 6, 128), jnp.float32),
            pltpu.VMEM((6, TGT_GROUP * MINE, 128), jnp.float32),
            pltpu.VMEM((2, 6, 8, 128), jnp.float32),
            pltpu.VMEM((TGT_GROUP, 8, 128), jnp.float32),
            pltpu.VMEM((TGT_GROUP, 8, 128), jnp.float32),
            dma((3,)),
            dma((15,)),
            dma((SRC_GROUP,)),
            dma((15,)),
            dma((SRC_GROUP,)),
            dma((7,)),
            dma((2 * NX,)),
            dma((7,)),
            dma((NZ,)),
            dma((7,)),
            dma((2 * NX,)),
            dma((7,)),
            dma((NZ,)),
            dma((TGT_GROUP,)),
            dma((TGT_GROUP,)),
        ],
        compiler_params=pltpu.CompilerParams(collective_id=0, has_side_effects=True),
    )(phase, mass.reshape(TILES, 128), active.reshape(1, MINE))
    return sums[0:3] * norming, sums[3:6] * norming


def solution(mesh):
    in_specs = (P(None, ("col", "row")), P(("col", "row")), P(("row", "col")))
    out_specs = (P(None, ("row", "col")), P(None, ("row", "col")))
    return jax.shard_map(shards, mesh=mesh, in_specs=in_specs, out_specs=out_specs, check_vma=False)
```

```python
import jax
import jax.numpy as jnp
from jax import lax
from jax.experimental import pallas as pl
from jax.experimental.pallas import tpu as pltpu
from jax.sharding import PartitionSpec as P

SOFTENING = 0.0001
MESH = pl.DeviceIdType.MESH

NX, NY, NZ = 4, 8, 8
SRC_GROUP = NY * 2
TGT_GROUP = NX * NZ
STARS = 1024
TILES = STARS // 128
MINE = 8
BATCH = 4


def remote(src, dst, send, recv, device):
    return pltpu.make_async_remote_copy(
        src_ref=src, dst_ref=dst, send_sem=send, recv_sem=recv, device_id=device, device_id_type=MESH
    )


def kernel(
    phase_ref, mass_ref, active_ref, out_ref,
    src, msrc, ids, idx_x, idx_z, pick_x, pick_z, tgt, raw, stage, part,
    own_sem, src_send, src_recv, mass_send, mass_recv, ix_send, ix_recv, iz_send, iz_recv,
    px_send, px_recv, pz_send, pz_recv, fin_send, fin_recv,
):
    rem, div = lax.rem, lax.div
    r, c = lax.axis_index("row"), lax.axis_index("col")
    z_lo, b = div(r, 16), rem(r, 16)
    y, core = div(b, 2), rem(b, 2)
    z_hi, x = div(c, NX), rem(c, NX)
    z = z_hi * 2 + z_lo
    m = z_lo * 16 + c
    slot = core * NX + x
    lane = lax.broadcasted_iota(jnp.int32, (8, 128), 1)

    def along_y(k, dc):
        bb = rem(y + k, NY) * 2 + (1 - core if dc else core)
        return (z_lo * 16 + bb, c), bb

    def along_x(k, dc):
        xx, cc = rem(x + k, NX), 1 - core if dc else core
        return (z_lo * 16 + y * 2 + cc, z_hi * NX + xx), cc * NX + xx

    def along_z(k):
        zz = rem(z + k, NZ)
        return (rem(zz, 2) * 16 + b, div(zz, 2) * NX + x), zz

    near = [along_y(k, 0) for k in (4, 3, 5, 2, 6, 1, 7)]
    beyond = [along_y(k, 1) for k in (4, 3, 5, 2, 6, 1, 7)]
    twin, twin_block = along_y(0, 1)
    across = [along_x(k, dc) for k, dc in ((2, 1), (2, 0), (1, 1), (3, 1), (1, 0), (3, 0), (0, 1))]
    fellows = [along_z(k) for k in (4, 3, 5, 2, 6, 1, 7)]
    partners = [d for d, _ in near + fellows + across]
    barrier = pltpu.get_barrier_semaphore()
    for device in partners:
        pl.semaphore_signal(barrier, inc=1, device_id=device, device_id_type=MESH)

    own = [
        pltpu.make_async_copy(active_ref, ids, own_sem.at[0]),
        pltpu.make_async_copy(phase_ref, src.at[b], own_sem.at[1]),
        pltpu.make_async_copy(mass_ref, msrc.at[b], own_sem.at[2]),
    ]
    for copy in own:
        copy.start()
    own[0].wait()
    idx_x[slot] = jnp.zeros((8, 128), jnp.int32)
    idx_x[slot, 0:1, 0:MINE] = ids[...]
    row = idx_x[slot, 0:1, :]
    for shift in (8, 16, 32, 64):
        row = row + pltpu.roll(row, shift, 1)
    idx_x[slot] = jnp.broadcast_to(row, (8, 128))

    pl.semaphore_wait(barrier, len(partners))

    sends = []

    def go(copy):
        copy.start()
        sends.append(copy)

    for n, (device, _) in enumerate(near):
        go(remote(phase_ref, src.at[b], src_send.at[n], src_recv.at[b], device))
    for n, (device, _) in enumerate(across):
        go(remote(idx_x.at[slot], idx_x.at[slot], ix_send.at[n], ix_recv.at[slot], device))
    go(remote(phase_ref, src.at[b], src_send.at[7], src_recv.at[b], twin))

    for device, ss in across:
        remote(idx_x.at[ss], idx_x.at[ss], ix_send.at[0], ix_recv.at[ss], device).wait_recv()
    sublane = lax.broadcasted_iota(jnp.int32, (8, 128), 0)
    merged = jnp.zeros((8, 128), jnp.int32)
    for cc in range(2):
        for xx in range(NX):
            chosen = (lane // MINE % NX == xx) & ((sublane == 0) == (cc == 0))
            merged = jnp.where(chosen, idx_x[cc * NX + xx], merged)
    idx_z[z] = merged
    for n, (device, _) in enumerate(fellows):
        go(remote(idx_z.at[z], idx_z.at[z], iz_send.at[n], iz_recv.at[z], device))
    for device, zz in fellows:
        remote(idx_z.at[zz], idx_z.at[zz], iz_send.at[0], iz_recv.at[zz], device).wait_recv()

    base = (c * 32 + z_lo * 16) * STARS
    within, tile = [], []
    for cc in range(2):
        for q in range(2):
            index = jnp.zeros((6, 128), jnp.int32)
            for h in range(NZ // 2):
                ids_h = jnp.broadcast_to(idx_z[h * 2 + q, cc:cc + 1, :], (6, 128))
                index = jnp.where(lane[:6] // 32 == h, ids_h, index)
            within.append((index - base) % 128)
            tile.append(lax.shift_right_arithmetic(index - base, 7))

    for n in (5, 6, 3, 4, 1, 2, 0):
        device, bb = near[n]
        remote(phase_ref, src.at[bb], src_send.at[0], src_recv.at[bb], device).wait_recv()
        go(remote(src.at[bb], src.at[bb], src_send.at[8 + n], src_recv.at[bb], twin))
    for copy in own[1:]:
        copy.wait()

    def choose(yy, found):
        found = list(found)
        bb = yy * 2 + core
        for k in range(TILES):
            piece = src[bb, :, k * 128:(k + 1) * 128]
            for n in range(4):
                values = jnp.take_along_axis(piece, within[n], axis=1)
                found[n] = jnp.where(tile[n] == bb * TILES + k, values, found[n])
        return tuple(found)

    found = lax.fori_loop(0, NY, choose, (jnp.zeros((6, 128), jnp.float32),) * 4)
    for n in range(4):
        pick_x[n // 2, slot, n % 2] = found[n]
    for n, (device, ss) in enumerate(across):
        cc = div(ss, NX)
        go(remote(pick_x.at[cc, slot], pick_x.at[cc, slot], px_send.at[n], px_recv.at[slot], device))
    early = len(sends)
    for n, (device, _) in enumerate(near + beyond + [(twin, 0)]):
        go(remote(mass_ref, msrc.at[b], mass_send.at[n], mass_recv.at[b], device))
    total = [pick_x[core, slot, q] for q in range(2)]
    for device, ss in across[::-1]:
        remote(pick_x.at[core, ss], pick_x.at[core, ss], px_send.at[0], px_recv.at[ss], device).wait_recv()
        for q in range(2):
            total[q] = total[q] + pick_x[core, ss, q]
    for q in range(2):
        pick_z[z, q] = total[q]
    for n, (device, _) in enumerate(fellows):
        go(remote(pick_z.at[z], pick_z.at[z], pz_send.at[n], pz_recv.at[z], device))
    for device, bb in [(twin, twin_block)] + beyond:
        remote(phase_ref, src.at[bb], src_send.at[0], src_recv.at[bb], twin).wait_recv()
    for device, bb in near + beyond + [(twin, twin_block)]:
        remote(mass_ref, msrc.at[bb], mass_send.at[0], mass_recv.at[bb], device).wait_recv()
    for copy in sends[:early]:
        copy.wait_send()
    for device, zz in fellows[::-1]:
        remote(pick_z.at[zz], pick_z.at[zz], pz_send.at[0], pz_recv.at[zz], device).wait_recv()
        for q in range(2):
            total[q] = total[q] + pick_z[zz, q]
    for q in range(2):
        turned = jnp.concatenate([total[q], jnp.zeros((2, 128), jnp.float32)], axis=0).T
        for k in range(6):
            tgt[k, q * 128:(q + 1) * 128, :] = jnp.broadcast_to(turned[:, k:k + 1], (128, 128))

    def owner(i):
        step, turn = div(i, 4), rem(i, 4)
        zz = rem(z + 4 + (1 - 2 * rem(step, 2)) * div(step + 1, 2), NZ)
        xx = rem(x + 2 + div(turn, 2) - rem(turn, 2) * (1 + div(turn, 2) * 2), NX)
        return zz, xx, rem(zz, 2) * 16 + div(zz, 2) * NX + xx

    def reduce(member):
        out = jnp.zeros((8, 128), jnp.float32)
        for n in range(6):
            value = raw[n] if n < 3 else raw[n] - 3.0 * raw[n + 3]
            out = jnp.where(lane == n, jnp.sum(value, axis=1, keepdims=True), out)
        stage[member] = out

    def hand_over(zz, xx, member):
        device = (rem(zz, 2) * 16 + b, div(zz, 2) * NX + xx)
        remote(stage.at[member], part.at[m], fin_send.at[member], fin_recv.at[m], device).start()

    def sweep(member):
        here = [tgt[k, pl.ds(pl.multiple_of(member * MINE, MINE), MINE), :] for k in range(6)]
        sums = [jnp.zeros((8, 128), jnp.float32)] * 9
        for t in range(SRC_GROUP * TILES):
            bb, k = t // TILES, t % TILES
            star = [jnp.broadcast_to(src[bb, n:n + 1, k * 128:(k + 1) * 128], (8, 128)) for n in range(6)]
            heft = jnp.broadcast_to(msrc[bb, k:k + 1, :], (8, 128))
            dx, dy, dz, du, dv, dw = (star[n] - here[n] for n in range(6))
            dist_sq = (dx * dx + dy * dy + dz * dz) + SOFTENING
            inverse = lax.rsqrt(dist_sq)
            inverse_sq = inverse * inverse
            weight = heft * inverse * inverse_sq
            third = (dx * du + dy * dv + dz * dw) * inverse_sq
            pull = (weight * dx, weight * dy, weight * dz)
            drag = (weight * du, weight * dv, weight * dw)
            for n in range(3):
                sums[n] += pull[n]
                sums[3 + n] += drag[n]
                sums[6 + n] += third * pull[n]
        for n in range(9):
            raw[n] = sums[n]

    def one(i, carry):
        reduce(carry[0])
        sweep(carry[1])
        return carry[1], owner(i + 1)[2]

    def batch(i, carry):
        carry = lax.fori_loop(i * BATCH, i * BATCH + BATCH, one, carry)

        @pl.when(i > 0)
        def _():
            hand_over(*owner(i * BATCH - 1))

        for j in range(BATCH - 1):
            hand_over(*owner(i * BATCH + j))
        return carry

    def last(i, carry):
        before, now = carry
        reduce(before[2])
        hand_over(*before)
        sweep(now[2])
        return now, owner(i + 1)

    raw[...] = jnp.zeros_like(raw)
    first = owner(0)[2]
    lax.fori_loop(0, TGT_GROUP // BATCH - 1, batch, (first, first))
    tail = TGT_GROUP - BATCH
    lax.fori_loop(tail, TGT_GROUP, last, (owner(tail - 1), owner(tail)))
    reduce(m)

    def sent(i, carry):
        member = owner(i)[2]
        remote(stage.at[member], part.at[member], fin_send.at[member], fin_recv.at[member], twin).wait_send()
        return carry

    def arrived(i, out):
        member = owner(i)[2]
        remote(stage.at[member], part.at[member], fin_send.at[member], fin_recv.at[member], twin).wait_recv()
        return out + part[member]

    for copy in sends[early:]:
        copy.wait_send()
    lax.fori_loop(0, tail, sent, 0)
    out = lax.fori_loop(0, TGT_GROUP - 1, arrived, stage[m])
    lax.fori_loop(tail, TGT_GROUP - 1, sent, 0)
    out_ref[...] = out.T[0:8, :]


def shards(phase, mass, active):
    norming = 1.0 / (phase.shape[1] * lax.axis_size("row") * lax.axis_size("col"))
    vmem = pl.BlockSpec(memory_space=pltpu.VMEM)
    hbm = pl.BlockSpec(memory_space=pl.ANY)
    dma = pltpu.SemaphoreType.DMA
    sums = pl.pallas_call(
        kernel,
        out_shape=jax.ShapeDtypeStruct((8, MINE), jnp.float32),
        in_specs=[hbm, hbm, hbm],
        out_specs=vmem,
        scratch_shapes=[
            pltpu.VMEM((SRC_GROUP, 6, STARS), jnp.float32),
            pltpu.VMEM((SRC_GROUP, TILES, 128), jnp.float32),
            pltpu.VMEM((1, MINE), jnp.int32),
            pltpu.VMEM((2 * NX, 8, 128), jnp.int32),
            pltpu.VMEM((NZ, 8, 128), jnp.int32),
            pltpu.VMEM((2, 2 * NX, 2, 6, 128), jnp.float32),
            pltpu.VMEM((NZ, 2, 6, 128), jnp.float32),
            pltpu.VMEM((6, TGT_GROUP * MINE, 128), jnp.float32),
            pltpu.VMEM((9, 8, 128), jnp.float32),
            pltpu.VMEM((TGT_GROUP, 8, 128), jnp.float32),
            pltpu.VMEM((TGT_GROUP, 8, 128), jnp.float32),
            dma((3,)),
            dma((15,)),
            dma((SRC_GROUP,)),
            dma((15,)),
            dma((SRC_GROUP,)),
            dma((7,)),
            dma((2 * NX,)),
            dma((7,)),
            dma((NZ,)),
            dma((7,)),
            dma((2 * NX,)),
            dma((7,)),
            dma((NZ,)),
            dma((TGT_GROUP,)),
            dma((TGT_GROUP,)),
        ],
        compiler_params=pltpu.CompilerParams(collective_id=0, has_side_effects=True),
    )(phase, mass.reshape(TILES, 128), active.reshape(1, MINE))
    return sums[0:3] * norming, sums[3:6] * norming


def solution(mesh):
    in_specs = (P(None, ("col", "row")), P(("col", "row")), P(("row", "col")))
    out_specs = (P(None, ("row", "col")), P(None, ("row", "col")))
    return jax.shard_map(shards, mesh=mesh, in_specs=in_specs, out_specs=out_specs, check_vma=False)
```

```python
import jax
import jax.numpy as jnp
from jax import lax
from jax.experimental import pallas as pl
from jax.experimental.pallas import tpu as pltpu
from jax.sharding import PartitionSpec as P

SOFTENING = 0.0001
MESH = pl.DeviceIdType.MESH

NX, NY, NZ = 4, 8, 8
SRC_GROUP = NY * 2
TGT_GROUP = NX * NZ
STARS = 1024
TILES = STARS // 128
MINE = 8
BATCH = 4


def remote(src, dst, send, recv, device):
    return pltpu.make_async_remote_copy(
        src_ref=src, dst_ref=dst, send_sem=send, recv_sem=recv, device_id=device, device_id_type=MESH
    )


def kernel(
    phase_ref, mass_ref, active_ref, out_ref,
    src, msrc, ids, idx_x, idx_z, pick_x, pick_z, tgt, raw, stage, part,
    own_sem, src_send, src_recv, mass_send, mass_recv, ix_send, ix_recv, iz_send, iz_recv,
    px_send, px_recv, pz_send, pz_recv, fin_send, fin_recv,
):
    rem, div = lax.rem, lax.div
    r, c = lax.axis_index("row"), lax.axis_index("col")
    z_lo, b = div(r, 16), rem(r, 16)
    y, core = div(b, 2), rem(b, 2)
    z_hi, x = div(c, NX), rem(c, NX)
    z = z_hi * 2 + z_lo
    m = z_lo * 16 + c
    slot = core * NX + x
    lane = lax.broadcasted_iota(jnp.int32, (8, 128), 1)

    def along_y(k, dc):
        bb = rem(y + k, NY) * 2 + (1 - core if dc else core)
        return (z_lo * 16 + bb, c), bb

    def along_x(k, dc):
        xx, cc = rem(x + k, NX), 1 - core if dc else core
        return (z_lo * 16 + y * 2 + cc, z_hi * NX + xx), cc * NX + xx

    def along_z(k):
        zz = rem(z + k, NZ)
        return (rem(zz, 2) * 16 + b, div(zz, 2) * NX + x), zz

    near = [along_y(k, 0) for k in (4, 3, 5, 2, 6, 1, 7)]
    beyond = [along_y(k, 1) for k in (4, 3, 5, 2, 6, 1, 7)]
    twin, twin_block = along_y(0, 1)
    across = [along_x(k, dc) for k, dc in ((2, 1), (2, 0), (1, 1), (3, 1), (1, 0), (3, 0), (0, 1))]
    fellows = [along_z(k) for k in (4, 3, 5, 2, 6, 1, 7)]
    partners = [d for d, _ in near + fellows + across]
    barrier = pltpu.get_barrier_semaphore()
    for device in partners:
        pl.semaphore_signal(barrier, inc=1, device_id=device, device_id_type=MESH)

    own = [
        pltpu.make_async_copy(active_ref, ids, own_sem.at[0]),
        pltpu.make_async_copy(phase_ref, src.at[b], own_sem.at[1]),
        pltpu.make_async_copy(mass_ref, msrc.at[b], own_sem.at[2]),
    ]
    for copy in own:
        copy.start()
    own[0].wait()
    idx_x[slot] = jnp.zeros((8, 128), jnp.int32)
    idx_x[slot, 0:1, 0:MINE] = ids[...]
    row = idx_x[slot, 0:1, :]
    for shift in (8, 16, 32, 64):
        row = row + pltpu.roll(row, shift, 1)
    idx_x[slot] = jnp.broadcast_to(row, (8, 128))

    pl.semaphore_wait(barrier, len(partners))

    sends = []

    def go(copy):
        copy.start()
        sends.append(copy)

    for n, (device, _) in enumerate(near):
        go(remote(phase_ref, src.at[b], src_send.at[n], src_recv.at[b], device))
    for n, (device, _) in enumerate(across):
        go(remote(idx_x.at[slot], idx_x.at[slot], ix_send.at[n], ix_recv.at[slot], device))
    go(remote(phase_ref, src.at[b], src_send.at[7], src_recv.at[b], twin))

    for device, ss in across:
        remote(idx_x.at[ss], idx_x.at[ss], ix_send.at[0], ix_recv.at[ss], device).wait_recv()
    sublane = lax.broadcasted_iota(jnp.int32, (8, 128), 0)
    merged = jnp.zeros((8, 128), jnp.int32)
    for cc in range(2):
        for xx in range(NX):
            chosen = (lane // MINE % NX == xx) & ((sublane == 0) == (cc == 0))
            merged = jnp.where(chosen, idx_x[cc * NX + xx], merged)
    idx_z[z] = merged
    for n, (device, _) in enumerate(fellows):
        go(remote(idx_z.at[z], idx_z.at[z], iz_send.at[n], iz_recv.at[z], device))
    for device, zz in fellows:
        remote(idx_z.at[zz], idx_z.at[zz], iz_send.at[0], iz_recv.at[zz], device).wait_recv()

    base = (c * 32 + z_lo * 16) * STARS
    within, tile = [], []
    for cc in range(2):
        for q in range(2):
            index = jnp.zeros((6, 128), jnp.int32)
            for h in range(NZ // 2):
                ids_h = jnp.broadcast_to(idx_z[h * 2 + q, cc:cc + 1, :], (6, 128))
                index = jnp.where(lane[:6] // 32 == h, ids_h, index)
            within.append((index - base) % 128)
            tile.append(lax.shift_right_arithmetic(index - base, 7))

    for n in (5, 6, 3, 4, 1, 2, 0):
        device, bb = near[n]
        remote(phase_ref, src.at[bb], src_send.at[0], src_recv.at[bb], device).wait_recv()
        go(remote(src.at[bb], src.at[bb], src_send.at[8 + n], src_recv.at[bb], twin))
    for copy in own[1:]:
        copy.wait()

    def choose(yy, found):
        found = list(found)
        bb = yy * 2 + core
        for k in range(TILES):
            piece = src[bb, :, k * 128:(k + 1) * 128]
            for n in range(4):
                values = jnp.take_along_axis(piece, within[n], axis=1)
                found[n] = jnp.where(tile[n] == bb * TILES + k, values, found[n])
        return tuple(found)

    found = lax.fori_loop(0, NY, choose, (jnp.zeros((6, 128), jnp.float32),) * 4)
    for n in range(4):
        pick_x[n // 2, slot, n % 2] = found[n]
    for n, (device, ss) in enumerate(across):
        cc = div(ss, NX)
        go(remote(pick_x.at[cc, slot], pick_x.at[cc, slot], px_send.at[n], px_recv.at[slot], device))
    early = len(sends)
    for n, (device, _) in enumerate(near + beyond + [(twin, 0)]):
        go(remote(mass_ref, msrc.at[b], mass_send.at[n], mass_recv.at[b], device))
    total = [pick_x[core, slot, q] for q in range(2)]
    for device, ss in across[::-1]:
        remote(pick_x.at[core, ss], pick_x.at[core, ss], px_send.at[0], px_recv.at[ss], device).wait_recv()
        for q in range(2):
            total[q] = total[q] + pick_x[core, ss, q]
    for q in range(2):
        pick_z[z, q] = total[q]
    for n, (device, _) in enumerate(fellows):
        go(remote(pick_z.at[z], pick_z.at[z], pz_send.at[n], pz_recv.at[z], device))
    for device, bb in [(twin, twin_block)] + beyond:
        remote(phase_ref, src.at[bb], src_send.at[0], src_recv.at[bb], twin).wait_recv()
    for device, bb in near + beyond + [(twin, twin_block)]:
        remote(mass_ref, msrc.at[bb], mass_send.at[0], mass_recv.at[bb], device).wait_recv()
    for copy in sends[:early]:
        copy.wait_send()
    for device, zz in fellows[::-1]:
        remote(pick_z.at[zz], pick_z.at[zz], pz_send.at[0], pz_recv.at[zz], device).wait_recv()
        for q in range(2):
            total[q] = total[q] + pick_z[zz, q]
    for q in range(2):
        turned = jnp.concatenate([total[q], jnp.zeros((2, 128), jnp.float32)], axis=0).T
        for k in range(6):
            tgt[k, q * 128:(q + 1) * 128, :] = jnp.broadcast_to(turned[:, k:k + 1], (128, 128))

    def owner(i):
        step, turn = div(i, 4), rem(i, 4)
        zz = rem(z + 4 + (1 - 2 * rem(step, 2)) * div(step + 1, 2), NZ)
        xx = rem(x + 2 + div(turn, 2) - rem(turn, 2) * (1 + div(turn, 2) * 2), NX)
        return zz, xx, rem(zz, 2) * 16 + div(zz, 2) * NX + xx

    def reduce(member):
        out = jnp.zeros((8, 128), jnp.float32)
        for n in range(6):
            value = raw[n] if n < 3 else raw[n] - 3.0 * raw[n + 3]
            out = jnp.where(lane == n, jnp.sum(value, axis=1, keepdims=True), out)
        stage[member] = out

    def hand_over(zz, xx, member):
        device = (rem(zz, 2) * 16 + b, div(zz, 2) * NX + xx)
        remote(stage.at[member], part.at[m], fin_send.at[member], fin_recv.at[m], device).start()

    def sweep(member):
        here = [tgt[k, pl.ds(pl.multiple_of(member * MINE, MINE), MINE), :] for k in range(6)]
        sums = [jnp.zeros((8, 128), jnp.float32)] * 9
        for t in range(SRC_GROUP * TILES):
            bb, k = t // TILES, t % TILES
            star = [jnp.broadcast_to(src[bb, n:n + 1, k * 128:(k + 1) * 128], (8, 128)) for n in range(6)]
            heft = jnp.broadcast_to(msrc[bb, k:k + 1, :], (8, 128))
            dx, dy, dz, du, dv, dw = (star[n] - here[n] for n in range(6))
            dist_sq = (dx * dx + dy * dy + dz * dz) + SOFTENING
            inverse = lax.rsqrt(dist_sq)
            inverse_sq = inverse * inverse
            weight = heft * inverse * inverse_sq
            third = (dx * du + dy * dv + dz * dw) * inverse_sq
            pull = (weight * dx, weight * dy, weight * dz)
            drag = (weight * du, weight * dv, weight * dw)
            for n in range(3):
                sums[n] += pull[n]
                sums[3 + n] += drag[n]
                sums[6 + n] += third * pull[n]
        for n in range(9):
            raw[n] = sums[n]

    def one(i, carry):
        reduce(carry[0])
        sweep(carry[1])
        return carry[1], owner(i + 1)[2]

    def batch(i, carry):
        carry = lax.fori_loop(i * BATCH, i * BATCH + BATCH, one, carry)

        @pl.when(i > 0)
        def _():
            hand_over(*owner(i * BATCH - 1))

        for j in range(BATCH - 1):
            hand_over(*owner(i * BATCH + j))
        return carry

    def last(i, carry):
        before, now = carry
        reduce(before[2])
        hand_over(*before)
        sweep(now[2])
        return now, owner(i + 1)

    raw[...] = jnp.zeros_like(raw)
    first = owner(0)[2]
    lax.fori_loop(0, TGT_GROUP // BATCH - 1, batch, (first, first))
    tail = TGT_GROUP - BATCH
    lax.fori_loop(tail, TGT_GROUP, last, (owner(tail - 1), owner(tail)))
    reduce(m)

    def sent(i, carry):
        member = owner(i)[2]
        remote(stage.at[member], part.at[member], fin_send.at[member], fin_recv.at[member], twin).wait_send()
        return carry

    def arrived(i, out):
        member = owner(i)[2]
        remote(stage.at[member], part.at[member], fin_send.at[member], fin_recv.at[member], twin).wait_recv()
        return out + part[member]

    for copy in sends[early:]:
        copy.wait_send()
    lax.fori_loop(0, tail, sent, 0)
    out = lax.fori_loop(0, TGT_GROUP - 1, arrived, stage[m])
    lax.fori_loop(tail, TGT_GROUP - 1, sent, 0)
    out_ref[...] = out.T[0:8, :]


def shards(phase, mass, active):
    norming = 1.0 / (phase.shape[1] * lax.axis_size("row") * lax.axis_size("col"))
    vmem = pl.BlockSpec(memory_space=pltpu.VMEM)
    hbm = pl.BlockSpec(memory_space=pl.ANY)
    dma = pltpu.SemaphoreType.DMA
    sums = pl.pallas_call(
        kernel,
        out_shape=pltpu.VMEM((8, MINE), jnp.float32),
        in_specs=[hbm, hbm, hbm],
        out_specs=vmem,
        scratch_shapes=[
            pltpu.VMEM((SRC_GROUP, 6, STARS), jnp.float32),
            pltpu.VMEM((SRC_GROUP, TILES, 128), jnp.float32),
            pltpu.VMEM((1, MINE), jnp.int32),
            pltpu.VMEM((2 * NX, 8, 128), jnp.int32),
            pltpu.VMEM((NZ, 8, 128), jnp.int32),
            pltpu.VMEM((2, 2 * NX, 2, 6, 128), jnp.float32),
            pltpu.VMEM((NZ, 2, 6, 128), jnp.float32),
            pltpu.VMEM((6, TGT_GROUP * MINE, 128), jnp.float32),
            pltpu.VMEM((9, 8, 128), jnp.float32),
            pltpu.VMEM((TGT_GROUP, 8, 128), jnp.float32),
            pltpu.VMEM((TGT_GROUP, 8, 128), jnp.float32),
            dma((3,)),
            dma((15,)),
            dma((SRC_GROUP,)),
            dma((15,)),
            dma((SRC_GROUP,)),
            dma((7,)),
            dma((2 * NX,)),
            dma((7,)),
            dma((NZ,)),
            dma((7,)),
            dma((2 * NX,)),
            dma((7,)),
            dma((NZ,)),
            dma((TGT_GROUP,)),
            dma((TGT_GROUP,)),
        ],
        compiler_params=pltpu.CompilerParams(collective_id=0, has_side_effects=True),
    )(phase, mass.reshape(TILES, 128), active.reshape(1, MINE))
    return sums[0:3] * norming, sums[3:6] * norming


def solution(mesh):
    in_specs = (P(None, ("col", "row")), P(("col", "row")), P(("row", "col")))
    out_specs = (P(None, ("row", "col")), P(None, ("row", "col")))
    return jax.shard_map(shards, mesh=mesh, in_specs=in_specs, out_specs=out_specs, check_vma=False)
```

```python
import jax
import jax.numpy as jnp
from jax import lax
from jax.experimental import pallas as pl
from jax.experimental.pallas import tpu as pltpu
from jax.sharding import PartitionSpec as P

SOFTENING = 0.0001
MESH = pl.DeviceIdType.MESH

NX, NY, NZ = 4, 8, 8
SRC_GROUP = NY * 2
TGT_GROUP = NX * NZ
STARS = 1024
TILES = STARS // 128
MINE = 8
BATCH = 4


def remote(src, dst, send, recv, device):
    return pltpu.make_async_remote_copy(
        src_ref=src, dst_ref=dst, send_sem=send, recv_sem=recv, device_id=device, device_id_type=MESH
    )


def kernel(
    phase_ref, mass_ref, active_ref, out_ref,
    src, msrc, ids, idx_x, idx_z, pick_x, pick_z, tgt, raw, stage, part,
    own_sem, src_send, src_recv, mass_send, mass_recv, ix_send, ix_recv, iz_send, iz_recv,
    px_send, px_recv, pz_send, pz_recv, fin_send, fin_recv,
):
    rem, div = lax.rem, lax.div
    r, c = lax.axis_index("row"), lax.axis_index("col")
    z_lo, b = div(r, 16), rem(r, 16)
    y, core = div(b, 2), rem(b, 2)
    z_hi, x = div(c, NX), rem(c, NX)
    z = z_hi * 2 + z_lo
    m = z_lo * 16 + c
    slot = core * NX + x
    lane = lax.broadcasted_iota(jnp.int32, (8, 128), 1)

    def along_y(k, dc):
        bb = rem(y + k, NY) * 2 + (1 - core if dc else core)
        return (z_lo * 16 + bb, c), bb

    def along_x(k, dc):
        xx, cc = rem(x + k, NX), 1 - core if dc else core
        return (z_lo * 16 + y * 2 + cc, z_hi * NX + xx), cc * NX + xx

    def along_z(k):
        zz = rem(z + k, NZ)
        return (rem(zz, 2) * 16 + b, div(zz, 2) * NX + x), zz

    near = [along_y(k, 0) for k in (4, 3, 5, 2, 6, 1, 7)]
    beyond = [along_y(k, 1) for k in (4, 3, 5, 2, 6, 1, 7)]
    twin, twin_block = along_y(0, 1)
    across = [along_x(k, dc) for k, dc in ((2, 1), (2, 0), (1, 1), (3, 1), (1, 0), (3, 0), (0, 1))]
    fellows = [along_z(k) for k in (4, 3, 5, 2, 6, 1, 7)]
    partners = [d for d, _ in near + fellows + across]
    barrier = pltpu.get_barrier_semaphore()
    for device in partners:
        pl.semaphore_signal(barrier, inc=1, device_id=device, device_id_type=MESH)

    own = [
        pltpu.make_async_copy(active_ref, ids, own_sem.at[0]),
        pltpu.make_async_copy(phase_ref, src.at[b], own_sem.at[1]),
        pltpu.make_async_copy(mass_ref, msrc.at[b], own_sem.at[2]),
    ]
    for copy in own:
        copy.start()
    own[0].wait()
    idx_x[slot] = jnp.zeros((8, 128), jnp.int32)
    idx_x[slot, 0:1, 0:MINE] = ids[...]
    row = idx_x[slot, 0:1, :]
    for shift in (8, 16, 32, 64):
        row = row + pltpu.roll(row, shift, 1)
    idx_x[slot] = jnp.broadcast_to(row, (8, 128))

    pl.semaphore_wait(barrier, len(partners))

    sends = []

    def go(copy):
        copy.start()
        sends.append(copy)

    for n, (device, _) in enumerate(near):
        go(remote(phase_ref, src.at[b], src_send.at[n], src_recv.at[b], device))
    for n, (device, _) in enumerate(across):
        go(remote(idx_x.at[slot], idx_x.at[slot], ix_send.at[n], ix_recv.at[slot], device))
    go(remote(phase_ref, src.at[b], src_send.at[7], src_recv.at[b], twin))

    for device, ss in across:
        remote(idx_x.at[ss], idx_x.at[ss], ix_send.at[0], ix_recv.at[ss], device).wait_recv()
    sublane = lax.broadcasted_iota(jnp.int32, (8, 128), 0)
    merged = jnp.zeros((8, 128), jnp.int32)
    for cc in range(2):
        for xx in range(NX):
            chosen = (lane // MINE % NX == xx) & ((sublane == 0) == (cc == 0))
            merged = jnp.where(chosen, idx_x[cc * NX + xx], merged)
    idx_z[z] = merged
    for n, (device, _) in enumerate(fellows):
        go(remote(idx_z.at[z], idx_z.at[z], iz_send.at[n], iz_recv.at[z], device))
    for device, zz in fellows:
        remote(idx_z.at[zz], idx_z.at[zz], iz_send.at[0], iz_recv.at[zz], device).wait_recv()

    base = (c * 32 + z_lo * 16) * STARS
    within, tile = [], []
    for cc in range(2):
        for q in range(2):
            index = jnp.zeros((6, 128), jnp.int32)
            for h in range(NZ // 2):
                ids_h = jnp.broadcast_to(idx_z[h * 2 + q, cc:cc + 1, :], (6, 128))
                index = jnp.where(lane[:6] // 32 == h, ids_h, index)
            within.append((index - base) % 128)
            tile.append(lax.shift_right_arithmetic(index - base, 7))

    for n in (5, 6, 3, 4, 1, 2, 0):
        device, bb = near[n]
        remote(phase_ref, src.at[bb], src_send.at[0], src_recv.at[bb], device).wait_recv()
        go(remote(src.at[bb], src.at[bb], src_send.at[8 + n], src_recv.at[bb], twin))
    for copy in own[1:]:
        copy.wait()

    def choose(yy, found):
        found = list(found)
        bb = yy * 2 + core
        for k in range(TILES):
            piece = src[bb, :, k * 128:(k + 1) * 128]
            for n in range(4):
                values = jnp.take_along_axis(piece, within[n], axis=1)
                found[n] = jnp.where(tile[n] == bb * TILES + k, values, found[n])
        return tuple(found)

    found = (jnp.zeros((6, 128), jnp.float32),) * 4
    for yy in range(NY):
        found = choose(yy, found)
    for n in range(4):
        pick_x[n // 2, slot, n % 2] = found[n]
    for n, (device, ss) in enumerate(across):
        cc = div(ss, NX)
        go(remote(pick_x.at[cc, slot], pick_x.at[cc, slot], px_send.at[n], px_recv.at[slot], device))
    early = len(sends)
    for n, (device, _) in enumerate(near + beyond + [(twin, 0)]):
        go(remote(mass_ref, msrc.at[b], mass_send.at[n], mass_recv.at[b], device))
    total = [pick_x[core, slot, q] for q in range(2)]
    for device, ss in across[::-1]:
        remote(pick_x.at[core, ss], pick_x.at[core, ss], px_send.at[0], px_recv.at[ss], device).wait_recv()
        for q in range(2):
            total[q] = total[q] + pick_x[core, ss, q]
    for q in range(2):
        pick_z[z, q] = total[q]
    for n, (device, _) in enumerate(fellows):
        go(remote(pick_z.at[z], pick_z.at[z], pz_send.at[n], pz_recv.at[z], device))
    for device, bb in [(twin, twin_block)] + beyond:
        remote(phase_ref, src.at[bb], src_send.at[0], src_recv.at[bb], twin).wait_recv()
    for device, bb in near + beyond + [(twin, twin_block)]:
        remote(mass_ref, msrc.at[bb], mass_send.at[0], mass_recv.at[bb], device).wait_recv()
    for copy in sends[:early]:
        copy.wait_send()
    for device, zz in fellows[::-1]:
        remote(pick_z.at[zz], pick_z.at[zz], pz_send.at[0], pz_recv.at[zz], device).wait_recv()
        for q in range(2):
            total[q] = total[q] + pick_z[zz, q]
    for q in range(2):
        turned = jnp.concatenate([total[q], jnp.zeros((2, 128), jnp.float32)], axis=0).T
        for k in range(6):
            tgt[k, q * 128:(q + 1) * 128, :] = jnp.broadcast_to(turned[:, k:k + 1], (128, 128))

    def owner(i):
        step, turn = div(i, 4), rem(i, 4)
        zz = rem(z + 4 + (1 - 2 * rem(step, 2)) * div(step + 1, 2), NZ)
        xx = rem(x + 2 + div(turn, 2) - rem(turn, 2) * (1 + div(turn, 2) * 2), NX)
        return zz, xx, rem(zz, 2) * 16 + div(zz, 2) * NX + xx

    def reduce(member):
        out = jnp.zeros((8, 128), jnp.float32)
        for n in range(6):
            value = raw[n] if n < 3 else raw[n] - 3.0 * raw[n + 3]
            out = jnp.where(lane == n, jnp.sum(value, axis=1, keepdims=True), out)
        stage[member] = out

    def hand_over(zz, xx, member):
        device = (rem(zz, 2) * 16 + b, div(zz, 2) * NX + xx)
        remote(stage.at[member], part.at[m], fin_send.at[member], fin_recv.at[m], device).start()

    def sweep(member):
        here = [tgt[k, pl.ds(pl.multiple_of(member * MINE, MINE), MINE), :] for k in range(6)]
        sums = [jnp.zeros((8, 128), jnp.float32)] * 9
        for t in range(SRC_GROUP * TILES):
            bb, k = t // TILES, t % TILES
            star = [jnp.broadcast_to(src[bb, n:n + 1, k * 128:(k + 1) * 128], (8, 128)) for n in range(6)]
            heft = jnp.broadcast_to(msrc[bb, k:k + 1, :], (8, 128))
            dx, dy, dz, du, dv, dw = (star[n] - here[n] for n in range(6))
            dist_sq = (dx * dx + dy * dy + dz * dz) + SOFTENING
            inverse = lax.rsqrt(dist_sq)
            inverse_sq = inverse * inverse
            weight = heft * inverse * inverse_sq
            third = (dx * du + dy * dv + dz * dw) * inverse_sq
            pull = (weight * dx, weight * dy, weight * dz)
            drag = (weight * du, weight * dv, weight * dw)
            for n in range(3):
                sums[n] += pull[n]
                sums[3 + n] += drag[n]
                sums[6 + n] += third * pull[n]
        for n in range(9):
            raw[n] = sums[n]

    def one(i, carry):
        reduce(carry[0])
        sweep(carry[1])
        return carry[1], owner(i + 1)[2]

    def batch(i, carry):
        carry = lax.fori_loop(i * BATCH, i * BATCH + BATCH, one, carry)

        @pl.when(i > 0)
        def _():
            hand_over(*owner(i * BATCH - 1))

        for j in range(BATCH - 1):
            hand_over(*owner(i * BATCH + j))
        return carry

    def last(i, carry):
        before, now = carry
        reduce(before[2])
        hand_over(*before)
        sweep(now[2])
        return now, owner(i + 1)

    raw[...] = jnp.zeros_like(raw)
    first = owner(0)[2]
    lax.fori_loop(0, TGT_GROUP // BATCH - 1, batch, (first, first))
    tail = TGT_GROUP - BATCH
    lax.fori_loop(tail, TGT_GROUP, last, (owner(tail - 1), owner(tail)))
    reduce(m)

    def sent(i, carry):
        member = owner(i)[2]
        remote(stage.at[member], part.at[member], fin_send.at[member], fin_recv.at[member], twin).wait_send()
        return carry

    def arrived(i, out):
        member = owner(i)[2]
        remote(stage.at[member], part.at[member], fin_send.at[member], fin_recv.at[member], twin).wait_recv()
        return out + part[member]

    for copy in sends[early:]:
        copy.wait_send()
    lax.fori_loop(0, tail, sent, 0)
    out = lax.fori_loop(0, TGT_GROUP - 1, arrived, stage[m])
    lax.fori_loop(tail, TGT_GROUP - 1, sent, 0)
    out_ref[...] = out.T[0:8, :]


def shards(phase, mass, active):
    norming = 1.0 / (phase.shape[1] * lax.axis_size("row") * lax.axis_size("col"))
    vmem = pl.BlockSpec(memory_space=pltpu.VMEM)
    hbm = pl.BlockSpec(memory_space=pl.ANY)
    dma = pltpu.SemaphoreType.DMA
    sums = pl.pallas_call(
        kernel,
        out_shape=pltpu.VMEM((8, MINE), jnp.float32),
        in_specs=[hbm, hbm, hbm],
        out_specs=vmem,
        scratch_shapes=[
            pltpu.VMEM((SRC_GROUP, 6, STARS), jnp.float32),
            pltpu.VMEM((SRC_GROUP, TILES, 128), jnp.float32),
            pltpu.VMEM((1, MINE), jnp.int32),
            pltpu.VMEM((2 * NX, 8, 128), jnp.int32),
            pltpu.VMEM((NZ, 8, 128), jnp.int32),
            pltpu.VMEM((2, 2 * NX, 2, 6, 128), jnp.float32),
            pltpu.VMEM((NZ, 2, 6, 128), jnp.float32),
            pltpu.VMEM((6, TGT_GROUP * MINE, 128), jnp.float32),
            pltpu.VMEM((9, 8, 128), jnp.float32),
            pltpu.VMEM((TGT_GROUP, 8, 128), jnp.float32),
            pltpu.VMEM((TGT_GROUP, 8, 128), jnp.float32),
            dma((3,)),
            dma((15,)),
            dma((SRC_GROUP,)),
            dma((15,)),
            dma((SRC_GROUP,)),
            dma((7,)),
            dma((2 * NX,)),
            dma((7,)),
            dma((NZ,)),
            dma((7,)),
            dma((2 * NX,)),
            dma((7,)),
            dma((NZ,)),
            dma((TGT_GROUP,)),
            dma((TGT_GROUP,)),
        ],
        compiler_params=pltpu.CompilerParams(collective_id=0, has_side_effects=True),
    )(phase, mass.reshape(TILES, 128), active.reshape(1, MINE))
    return sums[0:3] * norming, sums[3:6] * norming


def solution(mesh):
    in_specs = (P(None, ("col", "row")), P(("col", "row")), P(("row", "col")))
    out_specs = (P(None, ("row", "col")), P(None, ("row", "col")))
    return jax.shard_map(shards, mesh=mesh, in_specs=in_specs, out_specs=out_specs, check_vma=False)
```
